32 devices in a mesh: row: 4 (over y, x), col: 8 (over z, core).
Axes of the slice: x: 2, y: 2, z: 4, core: 2. Of those that a mesh axis runs over, the one named last changes fastest.
Arguments:
- panel_one: bfloat16 [16384, 2048], P(('row', 'col')), may hold values from -0.796875 to 0.796875
- panel_two: bfloat16 [16384, 2048], P(('row', 'col')), may hold values from -6 to 6
- inverse_one: bfloat16 [2048, 2048], P(None, 'col'), as said below
- inverse_two: bfloat16 [2048, 2048], P(None, 'col'), as said below
- update_list: int32 [32, 2], P(('row', 'col')), may hold values from -1 to 1, as said below
Outputs:
- factor_one: bfloat16 [16384, 2048], P(('row', 'col'))
- factor_two: bfloat16 [16384, 2048], P(('row', 'col'))
The draws below stay inside these ranges and needn't reach their ends.
Inputs may be any that keep to these rules, and one draw needn't show every extreme that they name: `inverse_one`: upper triangular: zero below the diagonal, diagonal entries between 0.5 and 1.5. `inverse_two`: upper triangular: zero below the diagonal, diagonal entries between 0.5 and 1.5. `update_list`: entry (d, j) names a block among the 2 first-supernode blocks of device d, or is -1 (no update). The named blocks of one device are distinct, a device's live entries come before its -1 entries, and every entry of devices 0 to 3 is live.
All inputs are finite; a program needn't handle non-finite values.
Results may differ from the reference program's by a relative error of at most 0.0056.
Values may be sent and summed in bfloat16 or wider, within the bound.
A program may use at most 128 MiB of HBM per device.

```python
import jax
import jax.numpy as jnp
from jax import lax

SN = 2048
B = 256
RB1 = 2
RB2 = 2
DEVS = 32
NCB = 8


def upper_factor(key):
    key_off, key_diag = jax.random.split(key)
    off = jax.random.normal(key_off, (SN, SN), jnp.float32) * SN ** (-0.5)
    diagonal = jax.random.uniform(key_diag, (SN,), jnp.float32, 0.5, 1.5)
    return (jnp.triu(off, 1) + jnp.diag(diagonal)).astype(jnp.bfloat16)


def draw_inverse_one(key, part):
    return upper_factor(jax.random.fold_in(key, 11))


def draw_inverse_two(key, part):
    return upper_factor(jax.random.fold_in(key, 23))


def draw_update_list(key, part):
    key_order, key_count = jax.random.split(jax.random.fold_in(key, 37))
    scores = jax.random.randint(key_order, (DEVS, RB1), 0, 1 << 20) * RB1 + jnp.arange(RB1, dtype=jnp.int32)[None, :]
    order = jnp.argsort(scores, axis=1, stable=True)[:, :RB2].astype(jnp.int32)
    counts = jax.random.randint(key_count, (DEVS, 1), 1, RB2 + 1)
    device_ids = jnp.arange(DEVS, dtype=jnp.int32)[:, None]
    counts = jnp.where(device_ids < NCB // RB2, RB2, counts)
    slots = jnp.arange(RB2, dtype=jnp.int32)[None, :]
    return jnp.where(slots < counts, order, -1).astype(jnp.int32)


def level_of(own_key, extent, cuts, smallest, high):
    def one(position, blocks):
        steps = jax.random.uniform(jax.random.fold_in(jax.random.fold_in(own_key, 6), position), (blocks,), jnp.float32, smallest / len(cuts), high / len(cuts))
        return jnp.repeat(jnp.exp(steps), extent[position] // blocks).reshape((-1,) + (1,) * (len(extent) - position - 1))

    loudness = one(*cuts[0])
    for cut in cuts[1:]:
        loudness = loudness * one(*cut)
    return loudness


def noise(key, extent, spread, reach, pieces=(), kind=jnp.bfloat16):
    result = jax.random.normal(key, extent, jnp.float32) * spread
    if len(pieces) > 0:
        result = level_of(key, extent, pieces, -0.22, 0.18) * result
    return jnp.clip(result, min=-reach, max=reach).astype(kind)


def setup_inputs(seed: int = 0) -> dict:
    keys = jax.random.split(jax.random.key(seed), 6)
    panel_one = noise(keys[0], (DEVS * RB1 * B, SN), 0.13, 0.796875, ((0, 32),))
    panel_two = noise(keys[1], (DEVS * RB2 * B, SN), 1.0, 6.0, ((0, 32),))
    inverse_one = draw_inverse_one(jax.random.fold_in(keys[5], 71), 0)
    inverse_two = draw_inverse_two(jax.random.fold_in(keys[5], 71), 0)
    update_list = draw_update_list(jax.random.fold_in(keys[5], 71), 0)
    return {"panel_one": panel_one, "panel_two": panel_two, "inverse_one": inverse_one, "inverse_two": inverse_two, "update_list": update_list}


def reference(panel_one, panel_two, inverse_one, inverse_two, update_list):
    factor_one = jnp.dot(panel_one, inverse_one, preferred_element_type=jnp.float32).astype(jnp.bfloat16)
    blocks = factor_one.reshape(DEVS * RB1, B, SN)
    device_base = (jnp.arange(DEVS, dtype=jnp.int32) * RB1)[:, None]
    source = (device_base + jnp.maximum(update_list, 0)).reshape(-1).astype(jnp.int32)
    living = (update_list >= 0).reshape(-1)
    chosen = blocks[source]
    selected = jnp.where(living[:, None, None], chosen, jnp.zeros((), chosen.dtype)).reshape(DEVS * RB2 * B, SN)
    column_panel = selected[:SN]
    update = lax.dot_general(selected, column_panel, (((1,), (1,)), ((), ())), preferred_element_type=jnp.float32)
    modified = (panel_two.astype(jnp.float32) - update).astype(jnp.bfloat16)
    factor_two = jnp.dot(modified, inverse_two, preferred_element_type=jnp.float32).astype(jnp.bfloat16)
    return factor_one, factor_two
```

```python
import functools

import jax
import jax.numpy as jnp
from jax import lax
from jax.experimental import pallas as pl
from jax.experimental.pallas import tpu as pltpu
from jax.sharding import PartitionSpec as P

MESH = pl.DeviceIdType.MESH
CORES = 2


def kernel(R, C, entries, p1, psel, p2, i1, i2, f1, f2, g1, g2, pg, cp, sel, mod, send, recv, local):
    Z = C // CORES
    T = R // 2
    rows, SN = p1.shape
    W = i1.shape[1]
    sources = pg.shape[0]
    order = [p ^ (p >> 1) for p in range(R)]
    row, col = lax.axis_index("row"), lax.axis_index("col")
    z, k = col // CORES, col % CORES
    pos, right, left = jnp.int32(0), jnp.int32(0), jnp.int32(0)
    for p in range(R):
        here = row == order[p]
        pos = jnp.where(here, p, pos)
        right = jnp.where(here, order[(p + 1) % R], right)
        left = jnp.where(here, order[(p + R - 1) % R], left)
    sibling = (row, z * CORES + 1 - k)

    items = [("i", zs, i1, g1, (zs + 1) * CORES * W) for zs in range(Z)]
    items += [("p", zs, psel, pg, rows) for zs in range(sources // CORES)]
    items += [("i", zs, i2, g2, (zs + 1) * CORES * W) for zs in range(Z)]
    pending = []

    def remote(src, dst, ssem, rsem, to):
        return pltpu.make_async_remote_copy(
            src_ref=src, dst_ref=dst, send_sem=ssem, recv_sem=rsem, device_id=to, device_id_type=MESH
        )

    def begin(when, make):
        def go():
            make().start()

        if when is None:
            go()
        else:
            pl.when(when)(go)
        pending.append((when, make))

    def arrive(when, dst, rsem):
        def go():
            remote(dst, dst, send.at[0, 0], rsem, sibling).wait_recv()

        if when is None:
            go()
        else:
            pl.when(when)(go)

    def piece(n, p, step, side):
        kind, zs, own, buf, H = items[n]
        h = H // R
        start, size = p * h, h
        if step == T:
            if h % 32 == 0:
                size = h // 2
                start = start + side * size
            elif side == 1:
                return None
        return buf.at[zs * CORES + k, pl.ds(pl.multiple_of(start, 8), size)]

    def active(n):
        return None if items[n][0] == "p" else z != items[n][1]

    def along_z(n, src):
        kind, zs, own, buf, H = items[n]
        for zd in range(Z):
            if zd != zs:
                begin(
                    z == zs,
                    lambda zd=zd: remote(
                        src, piece(n, pos, 0, 0), send.at[n, zd], recv.at[n, 0], (row, zd * CORES + k)
                    ),
                )

    def ring(n, step):
        base = Z + 2 * (step - 1)
        one = piece(n, lax.rem(pos + R - (step - 1), R), step, 0)
        two = piece(n, lax.rem(pos + step - 1, R), step, 1)
        for side, ref, to in ((0, one, right), (1, two, left)):
            if ref is not None:
                begin(
                    active(n),
                    lambda side=side, ref=ref, to=to: remote(
                        ref, ref, send.at[n, base + side], recv.at[n, 2 * step - 1 + side], (to, col)
                    ),
                )

    def ring_wait(n, step):
        one = piece(n, lax.rem(pos + R - step, R), step, 0)
        two = piece(n, lax.rem(pos + step, R), step, 1)
        for side, ref in ((0, one), (1, two)):
            if ref is not None:
                arrive(active(n), ref, recv.at[n, 2 * step - 1 + side])

    last_send, last_recv = Z + 2 * T, 2 * T + 1

    def whole(n, core):
        kind, zs, own, buf, H = items[n]
        return buf.at[zs * CORES + core, pl.ds(0, H)]

    def first(n):
        kind, zs, own, buf, H = items[n]
        if kind == "i":
            @pl.when(z == zs)
            def _():
                pltpu.make_async_copy(own.at[pl.ds(0, H)], whole(n, k), local.at[n]).start()

            h = H // R
            along_z(n, own.at[pl.ds(pl.multiple_of(pos * h, 8), h)])
            begin(
                z == zs,
                lambda: remote(
                    own.at[pl.ds(0, H)], whole(n, k), send.at[n, last_send], recv.at[n, last_recv], sibling
                ),
            )
        else:
            h = H // R
            origin = (z == zs) & (row == 0)

            @pl.when(origin)
            def _():
                pltpu.make_async_copy(
                    own.at[pl.ds(0, h)], buf.at[zs * CORES + k, pl.ds(0, h)], local.at[n]
                ).start()

            for p in range(1, R):
                begin(
                    origin,
                    lambda p=p: remote(
                        own.at[pl.ds(p * h, h)],
                        buf.at[zs * CORES + k, pl.ds(p * h, h)],
                        send.at[n, last_send + p],
                        recv.at[n, 0],
                        (order[p], col),
                    ),
                )

    def stage_a(n):
        kind, zs, own, buf, H = items[n]
        if kind == "i":
            arrive(z != zs, piece(n, pos, 0, 0), recv.at[n, 0])
        else:
            h = H // R
            origin = (z == zs) & (row == 0)

            @pl.when(origin)
            def _():
                pltpu.make_async_copy(
                    own.at[pl.ds(0, h)], buf.at[zs * CORES + k, pl.ds(0, h)], local.at[n]
                ).wait()

            arrive(jnp.logical_not(origin), piece(n, pos, 0, 0), recv.at[n, 0])
            along_z(n, piece(n, pos, 0, 0))
        ring(n, 1)

    def stage_b(n):
        for step in range(1, T):
            ring_wait(n, step)
            ring(n, step + 1)

    def stage_c(n):
        ring_wait(n, T)
        begin(
            active(n),
            lambda: remote(
                whole(n, k), whole(n, k), send.at[n, last_send], recv.at[n, last_recv], sibling
            ),
        )

    def stage_d(n):
        kind, zs, own, buf, H = items[n]
        arrive(None, whole(n, 1 - k), recv.at[n, last_recv])
        if kind == "i":
            @pl.when(z == zs)
            def _():
                pltpu.make_async_copy(own.at[pl.ds(0, H)], whole(n, k), local.at[n]).wait()

    def columns(out, left_of, buf, zs):
        for c in range(zs * CORES, (zs + 1) * CORES):
            depth = (c + 1) * W
            out[:, c * W:(c + 1) * W] = jnp.dot(
                left_of(depth), buf[c, 0:depth, :], preferred_element_type=jnp.float32
            ).astype(out.dtype)

    B = rows // entries.shape[1]

    def choose():
        for j in range(entries.shape[1]):
            entry = entries[0, j]
            value = jnp.zeros((B, SN), jnp.bfloat16)
            for b in range(entries.shape[1]):
                value = jnp.where(entry == b, f1[b * B:(b + 1) * B, :], value)
            sel[j * B:(j + 1) * B, :] = value

    def update(zs):
        for s in range(zs * CORES, (zs + 1) * CORES):
            for zz in range(Z):
                columns(cp, lambda depth: pg[s, :, 0:depth], g1, zz)
            span = rows // 2
            for half in range(2):
                product = lax.dot_general(
                    sel[...],
                    cp[half * span:(half + 1) * span, :],
                    (((1,), (1,)), ((), ())),
                    preferred_element_type=jnp.float32,
                )
                place = slice(s * rows + half * span, s * rows + (half + 1) * span)
                mod[:, place] = (p2[:, place].astype(jnp.float32) - product).astype(jnp.bfloat16)

    def compute(n):
        kind, zs, own, buf, H = items[n]
        if kind == "p":
            update(zs)
        elif n < Z:
            columns(f1, lambda depth: p1[:, 0:depth], g1, zs)
            if n == Z - 1:
                choose()
        else:
            columns(f2, lambda depth: mod[:, 0:depth], g2, zs)

    barrier = pltpu.get_barrier_semaphore()
    for d in range(1, R):
        pl.semaphore_signal(barrier, inc=1, device_id=(lax.rem(row + d, R), col), device_id_type=MESH)
    for d in range(1, Z):
        pl.semaphore_signal(
            barrier, inc=1, device_id=(row, lax.rem(z + d, Z) * CORES + k), device_id_type=MESH
        )
    pl.semaphore_signal(barrier, inc=1, device_id=sibling, device_id_type=MESH)
    pl.semaphore_wait(barrier, R - 1 + Z - 1 + 1)

    N = len(items)
    for n in range(N):
        if items[n][0] == "p":
            first(n)
    for n in range(N):
        if items[n][0] == "i":
            first(n)
    for t in range(N + 3):
        if t < N:
            stage_a(t)
        if 0 <= t - 1 < N:
            stage_b(t - 1)
        if 0 <= t - 2 < N:
            stage_c(t - 2)
        if 0 <= t - 3 < N:
            stage_d(t - 3)
            compute(t - 3)
    for when, make in pending:
        if when is None:
            make().wait_send()
        else:
            pl.when(when)(lambda make=make: make().wait_send())


def body(R, C, panel_one, panel_two, inverse_one, inverse_two, update_list):
    rows, SN = panel_one.shape
    W = inverse_one.shape[1]
    count = update_list.shape[1]
    B = rows // count
    entries = update_list[0]
    blocks = panel_one.reshape(count, B, SN)
    chosen = jnp.zeros((count, B, SN), jnp.bfloat16)
    for b in range(count):
        chosen = jnp.where((entries == b)[:, None, None], blocks[b][None], chosen)
    chosen = chosen.reshape(rows, SN)
    sources = SN // rows
    items = 2 * (C // CORES) + sources // CORES
    vmem = pl.BlockSpec(memory_space=pltpu.VMEM)
    return pl.pallas_call(
        functools.partial(kernel, R, C),
        out_shape=[jax.ShapeDtypeStruct((rows, SN), jnp.bfloat16)] * 2,
        in_specs=[pl.BlockSpec(memory_space=pltpu.SMEM)] + [vmem] * 5,
        out_specs=[vmem, vmem],
        scratch_shapes=[
            pltpu.VMEM((C, SN, W), jnp.bfloat16),
            pltpu.VMEM((C, SN, W), jnp.bfloat16),
            pltpu.VMEM((sources, rows, SN), jnp.bfloat16),
            pltpu.VMEM((rows, SN), jnp.bfloat16),
            pltpu.VMEM((rows, SN), jnp.bfloat16),
            pltpu.VMEM((rows, SN), jnp.bfloat16),
            pltpu.SemaphoreType.DMA((items, C // CORES + 2 * (R // 2) + R)),
            pltpu.SemaphoreType.DMA((items, 2 * (R // 2) + 2)),
            pltpu.SemaphoreType.DMA((items,)),
        ],
        compiler_params=pltpu.CompilerParams(
            collective_id=0, has_side_effects=True, vmem_limit_bytes=62 * 1024 * 1024
        ),
        name="panel",
    )(update_list, panel_one, chosen, panel_two, inverse_one, inverse_two)


def solution(mesh):
    R, C = mesh.shape["row"], mesh.shape["col"]
    return jax.shard_map(
        functools.partial(body, R, C),
        mesh=mesh,
        in_specs=(
            P(("row", "col"), None),
            P(("row", "col"), None),
            P(None, "col"),
            P(None, "col"),
            P(("row", "col"), None),
        ),
        out_specs=(P(("row", "col"), None), P(("row", "col"), None)),
        check_vma=False,
    )
```

```python
import functools

import jax
import jax.numpy as jnp
from jax import lax
from jax.experimental import pallas as pl
from jax.experimental.pallas import tpu as pltpu
from jax.sharding import PartitionSpec as P

MESH = pl.DeviceIdType.MESH
CORES = 2
SUBS = 4


def kernel(
    R, C, entries, h1, psel, h2, i1, i2, out1, out2, p1, p2, f1, f2, g1, g2, pg, cp, sel, mod, send, recv, local, moves
):
    Z = C // CORES
    T = R // 2
    rows, SN = p1.shape
    W = i1.shape[1]
    sources = pg.shape[0]
    order = [p ^ (p >> 1) for p in range(R)]
    row, col = lax.axis_index("row"), lax.axis_index("col")
    z, k = col // CORES, col % CORES
    pos, right, left = jnp.int32(0), jnp.int32(0), jnp.int32(0)
    for p in range(R):
        here = row == order[p]
        pos = jnp.where(here, p, pos)
        right = jnp.where(here, order[(p + 1) % R], right)
        left = jnp.where(here, order[(p + R - 1) % R], left)
    sibling = (row, z * CORES + 1 - k)

    items = [("i", zs, i1, g1, 0, (zs + 1) * CORES * W) for zs in range(Z)]
    planes = sources // CORES
    span = rows // SUBS
    items += [("p", zs, psel, pg, b * span, span) for b in range(SUBS) for zs in range(planes)]
    items += [("i", zs, i2, g2, 0, (zs + 1) * CORES * W) for zs in range(Z)]
    pending = []

    def remote(src, dst, ssem, rsem, to):
        return pltpu.make_async_remote_copy(
            src_ref=src, dst_ref=dst, send_sem=ssem, recv_sem=rsem, device_id=to, device_id_type=MESH
        )

    def begin(when, make):
        def go():
            make().start()

        if when is None:
            go()
        else:
            pl.when(when)(go)
        pending.append((when, make))

    def arrive(when, dst, rsem):
        def go():
            remote(dst, dst, send.at[0, 0], rsem, sibling).wait_recv()

        if when is None:
            go()
        else:
            pl.when(when)(go)

    def piece(n, p, step, side):
        kind, zs, own, buf, base, H = items[n]
        h = H // R
        start, size = base + p * h, h
        if step == T:
            if h % 32 == 0:
                size = h // 2
                start = start + side * size
            elif side == 1:
                return None
        return buf.at[zs * CORES + k, pl.ds(pl.multiple_of(start, 8), size)]

    def active(n):
        return z != items[n][1]

    def along_z(n, src, when):
        zs = items[n][1]
        if zs > 0:
            begin(
                when,
                lambda: remote(src, piece(n, pos, 0, 0), send.at[n, 0], recv.at[n, 0], (row, col - CORES)),
            )
        if zs < Z - 1:
            begin(
                when,
                lambda: remote(src, piece(n, pos, 0, 0), send.at[n, 1], recv.at[n, 0], (row, col + CORES)),
            )

    def onward(n):
        zs = items[n][1]
        ref = piece(n, pos, 0, 0)
        if zs > 1:
            begin(
                (z < zs) & (z > 0),
                lambda: remote(ref, ref, send.at[n, 0], recv.at[n, 0], (row, col - CORES)),
            )
        if zs < Z - 2:
            begin(
                (z > zs) & (z < Z - 1),
                lambda: remote(ref, ref, send.at[n, 1], recv.at[n, 0], (row, col + CORES)),
            )

    def ring(n, step):
        base = 2 + 2 * (step - 1)
        one = piece(n, lax.rem(pos + R - (step - 1), R), step, 0)
        two = piece(n, lax.rem(pos + step - 1, R), step, 1)
        for side, ref, to in ((0, one, right), (1, two, left)):
            if ref is not None:
                begin(
                    active(n),
                    lambda side=side, ref=ref, to=to: remote(
                        ref, ref, send.at[n, base + side], recv.at[n, 2 * step - 1 + side], (to, col)
                    ),
                )

    def ring_wait(n, step):
        one = piece(n, lax.rem(pos + R - step, R), step, 0)
        two = piece(n, lax.rem(pos + step, R), step, 1)
        for side, ref in ((0, one), (1, two)):
            if ref is not None:
                arrive(active(n), ref, recv.at[n, 2 * step - 1 + side])

    last_send, last_recv = 2 + 2 * T, 2 * T + 1

    def whole(n, core):
        kind, zs, own, buf, base, H = items[n]
        return buf.at[zs * CORES + core, pl.ds(base, H)]

    def load_own(n):
        kind, zs, own, buf, base, H = items[n]
        return pltpu.make_async_copy(own.at[pl.ds(base, H)], whole(n, k), local.at[n])

    def first(n):
        kind, zs, own, buf, base, H = items[n]
        h = H // R
        if kind == "i":
            along_z(n, own.at[pl.ds(pl.multiple_of(pos * h, 8), h)], z == zs)
            begin(
                z == zs,
                lambda: remote(
                    own.at[pl.ds(0, H)], whole(n, k), send.at[n, last_send], recv.at[n, last_recv], sibling
                ),
            )
            pl.when(z == zs)(lambda: load_own(n).start())
        else:
            origin = (z == zs) & (pos == 0)
            for side, to in ((0, right), (1, left)):
                begin(
                    origin,
                    lambda side=side, to=to: remote(
                        own.at[pl.ds(base + side * (H // 2), H // 2)],
                        half(n, side),
                        send.at[n, 2 + side],
                        recv.at[n, 1 + side],
                        (to, col),
                    ),
                )
            along_z(n, own.at[pl.ds(base, h)], origin)
            begin(
                origin,
                lambda: remote(
                    own.at[pl.ds(base, H)], whole(n, k), send.at[n, last_send], recv.at[n, last_recv], sibling
                ),
            )
            pl.when(origin)(lambda: load_own(n).start())

    def half(n, side):
        kind, zs, own, buf, base, H = items[n]
        return buf.at[zs * CORES + k, pl.ds(base + side * (H // 2), H // 2)]

    def hop(n, h):
        zs = items[n][1]
        for side, at, to in ((0, h, right), (1, R - h, left)):
            when = (z == zs) & (pos == at)
            arrive(when, half(n, side), recv.at[n, 1 + side])
            if h < R - 1:
                begin(
                    when,
                    lambda side=side, to=to: remote(
                        half(n, side), half(n, side), send.at[n, 2 + side], recv.at[n, 1 + side], (to, col)
                    ),
                )
        if h == T:
            along_z(n, piece(n, pos, 0, 0), (z == zs) & (pos == h))
        elif h < T:
            along_z(n, piece(n, pos, 0, 0), (z == zs) & ((pos == h) | (pos == R - h)))
        if h == R - 1:
            begin(
                (z == zs) & (pos != 0),
                lambda: remote(
                    whole(n, k), whole(n, k), send.at[n, last_send], recv.at[n, last_recv], sibling
                ),
            )

    def stage_a(n):
        arrive(active(n), piece(n, pos, 0, 0), recv.at[n, 0])
        onward(n)
        ring(n, 1)

    def stage_b(n):
        for step in range(1, T):
            ring_wait(n, step)
            ring(n, step + 1)

    def stage_c(n):
        ring_wait(n, T)
        begin(
            active(n),
            lambda: remote(
                whole(n, k), whole(n, k), send.at[n, last_send], recv.at[n, last_recv], sibling
            ),
        )

    def stage_d(n):
        kind, zs, own, buf, base, H = items[n]
        arrive(None, whole(n, 1 - k), recv.at[n, last_recv])
        pl.when((z == zs) if kind == "i" else (z == zs) & (pos == 0))(lambda: load_own(n).wait())

    def columns(out, left_of, buf, zs):
        for c in range(zs * CORES, (zs + 1) * CORES):
            depth = (c + 1) * W
            out[:, c * W:(c + 1) * W] = jnp.dot(
                left_of(depth), buf[c, 0:depth, :], preferred_element_type=jnp.float32
            ).astype(out.dtype)

    B = rows // entries.shape[1]

    def choose():
        for j in range(entries.shape[1]):
            entry = entries[0, j]
            value = jnp.zeros((B, SN), jnp.bfloat16)
            for b in range(entries.shape[1]):
                value = jnp.where(entry == b, f1[b * B:(b + 1) * B, :], value)
            sel[j * B:(j + 1) * B, :] = value

    def update(s):
        for zz in range(Z):
            columns(cp, lambda depth: pg[s, :, 0:depth], g1, zz)
        width = rows // 2
        for part in range(2):
            product = lax.dot_general(
                sel[...],
                cp[part * width:(part + 1) * width, :],
                (((1,), (1,)), ((), ())),
                preferred_element_type=jnp.float32,
            )
            place = slice(s * rows + part * width, s * rows + (part + 1) * width)
            mod[:, place] = (p2[:, place].astype(jnp.float32) - product).astype(jnp.bfloat16)

    def factor_one(n):
        if n == 0:
            loads[0].wait()
        columns(f1, lambda depth: p1[:, 0:depth], g1, items[n][1])
        if n == Z - 1:
            stores[0].start()
            choose()
            loads[1].wait()

    def store_two(zs):
        place = pl.ds(zs * CORES * W, CORES * W)
        return pltpu.make_async_copy(f2.at[:, place], out2.at[:, place], moves.at[3 + zs])

    def factor_two(n):
        zs = items[n][1]
        columns(f2, lambda depth: mod[:, 0:depth], g2, zs)
        store_two(zs).start()

    loads = [pltpu.make_async_copy(h1, p1, moves.at[0]), pltpu.make_async_copy(h2, p2, moves.at[1])]
    stores = [pltpu.make_async_copy(f1, out1, moves.at[2])]

    barrier = pltpu.get_barrier_semaphore()
    for d in range(1, R):
        pl.semaphore_signal(barrier, inc=1, device_id=(lax.rem(row + d, R), col), device_id_type=MESH)
    for d in range(1, Z):
        pl.semaphore_signal(
            barrier, inc=1, device_id=(row, lax.rem(z + d, Z) * CORES + k), device_id_type=MESH
        )
    pl.semaphore_signal(barrier, inc=1, device_id=sibling, device_id_type=MESH)
    pl.semaphore_wait(barrier, R - 1 + Z - 1 + 1)

    N = len(items)
    P0, Q0 = Z, Z + SUBS * planes
    for n in list(range(P0, Q0)) + list(range(P0)):
        first(n)
    for load in loads:
        load.start()
    events = []
    for i in range(Z):
        events.append((0.5, first, Q0 + i))
        for stage, extra in ((stage_a, 0), (stage_b, 4), (stage_c, 7), (stage_d, 9), (factor_one, 9.1)):
            events.append((1 + i * (i + 5) / 3 + extra, stage, i))
    for b in range(SUBS):
        for zs in range(planes):
            n = P0 + b * planes + zs
            for h in range(1, R):
                events.append((4 * b + 4 * h, functools.partial(hop, h=h), n))
            for stage, extra in ((stage_a, 12), (stage_b, 16), (stage_c, 20), (stage_d, 24)):
                events.append((4 * b + extra, stage, n))
    for s in range(sources):
        events.append((4 * SUBS + 21 + s, update, s))
    for i in range(Z):
        n = Q0 + i
        for stage, key in ((stage_a, 11 + i * (i + 5) * 2 / 3), (stage_b, 15 + i * (i + 6) * 2 / 3), (stage_c, 18 + i * (i + 6) * 2 / 3)):
            events.append((key, stage, n))
        for stage, key in ((stage_d, 60 + i), (factor_two, 60.1 + i)):
            events.append((key, stage, n))
    for _, stage, n in sorted(events, key=lambda event: event[0]):
        stage(n)
    stores[0].wait()
    for zs in range(Z):
        store_two(zs).wait()
    for when, make in pending:
        if when is None:
            make().wait_send()
        else:
            pl.when(when)(lambda make=make: make().wait_send())


def body(R, C, panel_one, panel_two, inverse_one, inverse_two, update_list):
    rows, SN = panel_one.shape
    W = inverse_one.shape[1]
    count = update_list.shape[1]
    B = rows // count
    entries = update_list[0]
    blocks = panel_one.reshape(count, B, SN)
    chosen = jnp.zeros((count, B, SN), jnp.bfloat16)
    for b in range(count):
        chosen = jnp.where((entries == b)[:, None, None], blocks[b][None], chosen)
    chosen = chosen.reshape(rows, SN)
    sources = SN // rows
    items = 2 * (C // CORES) + SUBS * (sources // CORES)
    hbm = pl.BlockSpec(memory_space=pl.ANY)
    return pl.pallas_call(
        functools.partial(kernel, R, C),
        out_shape=[jax.ShapeDtypeStruct((rows, SN), jnp.bfloat16)] * 2,
        in_specs=[pl.BlockSpec(memory_space=pltpu.SMEM)] + [hbm] * 5,
        out_specs=[hbm, hbm],
        scratch_shapes=[pltpu.VMEM((rows, SN), jnp.bfloat16) for _ in range(4)]
        + [
            pltpu.VMEM((C, SN, W), jnp.bfloat16),
            pltpu.VMEM((C, SN, W), jnp.bfloat16),
            pltpu.VMEM((sources, rows, SN), jnp.bfloat16),
            pltpu.VMEM((rows, SN), jnp.bfloat16),
            pltpu.VMEM((rows, SN), jnp.bfloat16),
            pltpu.VMEM((rows, SN), jnp.bfloat16),
            pltpu.SemaphoreType.DMA((items, 3 + 2 * (R // 2))),
            pltpu.SemaphoreType.DMA((items, 2 * (R // 2) + 2)),
            pltpu.SemaphoreType.DMA((items,)),
            pltpu.SemaphoreType.DMA((3 + C // CORES,)),
        ],
        compiler_params=pltpu.CompilerParams(
            collective_id=0, has_side_effects=True, vmem_limit_bytes=62 * 1024 * 1024
        ),
        name="panel",
    )(update_list, panel_one, chosen, panel_two, inverse_one, inverse_two)


def solution(mesh):
    R, C = mesh.shape["row"], mesh.shape["col"]
    return jax.shard_map(
        functools.partial(body, R, C),
        mesh=mesh,
        in_specs=(
            P(("row", "col"), None),
            P(("row", "col"), None),
            P(None, "col"),
            P(None, "col"),
            P(("row", "col"), None),
        ),
        out_specs=(P(("row", "col"), None), P(("row", "col"), None)),
        check_vma=False,
    )
```
